32 devices in a mesh: kz: 4 (over x, core), en: 2 (over y), sp: 4 (over z).
Axes of the slice: x: 2, y: 2, z: 4, core: 2. Of those that a mesh axis runs over, the one named last changes fastest.
Arguments:
- green: float32 [4, 4, 4, 2, 256, 256], P('kz', 'en', 'sp'), may hold values from -0.1 to 0.1
- coupling: float32 [4, 3, 256, 256], P('sp'), may hold values from -0.375 to 0.375
- phonon_weight: float32 [3], replicated, may hold values from 0.2 to 0.6
- mode_index: int32 [4, 5], P('kz'), may hold values from 0 to 2
- onsite: float32 [4, 256], P('sp'), may hold values from 0.8 to 1.2
- hopping: float32 [4, 256], P('sp'), may hold values from 0.45 to 0.95
- energies: float32 [4], P('en'), may hold values from -0.1 to 0.1
- guess_scale: float32 [4, 4, 4], P('kz', 'en', 'sp'), may hold values from 0.45 to 0.75
Outputs:
- boundary: float32 [4, 4, 4, 2, 256, 256], P('kz', 'en', 'sp')
The draws below stay inside these ranges and needn't reach their ends.
All inputs are finite; a program needn't handle non-finite values.
Results may differ from the reference program's by a relative error of at most 0.0003.
Values sent between devices are 32-bit elements; how exact they have to be, the bound alone decides.
A program may use at most 64 MiB of HBM per device.

```python
import math
import jax
import jax.numpy as jnp
from jax import lax

NB = 256
MODES = 3
REACH = 2
NEWTON = 3
KZ = 4
NE = 4
NSLAB = 4


def plant(values, rng, least, largest):
    spot = [jax.random.randint(jax.random.fold_in(rng, axis), (), 0, length) for axis, length in enumerate(values.shape)]
    main_axis = values.shape.index(max(values.shape))
    next_to = spot[:main_axis] + [(spot[main_axis] + 1) % values.shape[main_axis]] + spot[main_axis + 1:]
    return values.at[tuple(spot)].set(least).at[tuple(next_to)].set(largest)


def steps_of(rng, extent, shards, low, largest):
    def one(axis_at, blocks):
        draws = jax.random.uniform(jax.random.fold_in(jax.random.fold_in(rng, 6), axis_at), (blocks,), jnp.float32, low / len(shards), largest / len(shards))
        return jnp.repeat(jnp.exp(draws), extent[axis_at] // blocks).reshape((-1,) + (1,) * (len(extent) - axis_at - 1))

    gain = one(*shards[0])
    for cut in shards[1:]:
        gain = gain * one(*cut)
    return gain


def bell_draw(own_key, shape, scale, most, shards=(), held_as=jnp.bfloat16):
    gain = steps_of(own_key, shape, shards, -0.22, 0.18) if shards else 1.0
    values = jax.random.normal(own_key, shape, jnp.float32) * scale * gain
    return jnp.minimum(jnp.maximum(values, -most), most).astype(held_as)


def setup_inputs(seed: int = 0) -> dict:
    arg_keys = jax.random.split(jax.random.key(seed), 9)
    return {
        "green": bell_draw(arg_keys[0], (KZ, NE, NSLAB, 2, NB, NB), 0.012, 0.1, ((0, 4), (1, 2), (2, 4)), jnp.float32),
        "coupling": bell_draw(arg_keys[1], (NSLAB, MODES, NB, NB), NB ** -0.5, 0.375, ((0, 4),), jnp.float32),
        "phonon_weight": jnp.clip(jnp.exp(jax.random.uniform(arg_keys[2], (MODES,), jnp.float32, math.log(0.2), math.log(0.6))), 0.2, 0.6),
        "mode_index": plant(jax.random.randint(arg_keys[3], (KZ, 2 * REACH + 1), 0, MODES), jax.random.fold_in(arg_keys[3], 1), 0, MODES - 1).astype(jnp.int32),
        "onsite": jnp.clip(0.8 + 0.40000004 * jax.random.uniform(arg_keys[4], (NSLAB, NB), jnp.float32) ** steps_of(arg_keys[4], (NSLAB, NB), ((0, 4),), -0.2, 0.2), 0.8, 1.2),
        "hopping": jnp.clip(jnp.exp(math.log(0.95) - 0.74721442 * jax.random.uniform(arg_keys[5], (NSLAB, NB), jnp.float32) ** steps_of(arg_keys[5], (NSLAB, NB), ((0, 4),), -0.2, 0.2)), 0.45, 0.95),
        "energies": jnp.clip(jax.random.uniform(arg_keys[6], (NE,), jnp.float32, -0.1, 0.1) * steps_of(arg_keys[6], (NE,), ((0, 2),), -0.4, 0.0), -0.1, 0.1),
        "guess_scale": jnp.clip(0.45 + 0.3 * jax.random.uniform(arg_keys[7], (KZ, NE, NSLAB), jnp.float32) ** steps_of(arg_keys[7], (KZ, NE, NSLAB), ((0, 4), (1, 2), (2, 4)), -0.2, 0.2), 0.45, 0.75),
    }


HIGHEST_PRECISION = lax.Precision.HIGHEST


def sandwich(matrix, blocks):
    left_product = jnp.einsum('ab,nbc->nac', matrix, blocks, precision=HIGHEST_PRECISION)
    return jnp.einsum('nac,dc->nad', left_product, matrix, precision=HIGHEST_PRECISION)


def batched(first, second):
    return jnp.einsum('...ab,...bc->...ac', first, second, precision=HIGHEST_PRECISION)


def reference(green, coupling, phonon_weight, mode_index, onsite, hopping, energies, guess_scale):
    mode_range = jnp.arange(MODES, dtype=jnp.int32)
    identity = jnp.eye(NB, dtype=jnp.float32)

    def slab_step(boundary, inputs):
        green_slab, couplings, onsite_slab, hop_slab, guess_slab = inputs
        scattered = jnp.zeros(green_slab.shape, jnp.float32)
        for column in range(2 * REACH + 1):
            offset = column - REACH
            shifted = jnp.roll(green_slab, offset, axis=0)

            def per_point(pair):
                index_row, blocks = pair
                selector = (index_row[column] == mode_range).astype(jnp.float32)
                matrix = jnp.sum(selector[:, None, None] * couplings, axis=0)
                weight = jnp.sum(selector * phonon_weight)
                flat = blocks.reshape(-1, NB, NB)
                return (weight * sandwich(matrix, flat)).reshape(blocks.shape)

            scattered = scattered + lax.map(per_point, (mode_index, shifted))
        padded = jnp.pad(scattered, ((0, 0), (1, 1), (0, 0), (0, 0), (0, 0)))
        self_energy = padded[:, :-2] + padded[:, 2:]
        diagonal_shift = onsite_slab[None, :] - energies[:, None]
        system_re = self_energy[:, :, 0] + identity * diagonal_shift[None, :, None, :]
        system_im = self_energy[:, :, 1]
        guess = guess_slab[:, :, None, None]
        inverse_re = 2.0 * guess * identity - guess * guess * system_re
        inverse_im = -(guess * guess) * system_im
        for step in range(NEWTON - 1):
            product_re = batched(system_re, inverse_re) - batched(system_im, inverse_im)
            product_im = batched(system_re, inverse_im) + batched(system_im, inverse_re)
            residual_re = 2.0 * identity - product_re
            residual_im = -product_im
            inverse_re, inverse_im = (batched(inverse_re, residual_re) - batched(inverse_im, residual_im),
                                      batched(inverse_re, residual_im) + batched(inverse_im, residual_re))
        inverse = jnp.stack([inverse_re, inverse_im], axis=2)
        outer_hop = hop_slab[:, None] * hop_slab[None, :]
        boundary = outer_hop * boundary + inverse
        return boundary, boundary

    start = jnp.zeros((KZ, NE, 2, NB, NB), jnp.float32)
    inputs = (jnp.moveaxis(green, 2, 0), coupling, onsite, hopping, jnp.moveaxis(guess_scale, 2, 0))
    final_state, stacked = lax.scan(slab_step, start, inputs)
    return jnp.moveaxis(stacked, 0, 2)
```

```python
import functools

import jax
import jax.numpy as jnp
from jax import lax
from jax.experimental import pallas as pl
from jax.experimental.pallas import tpu as pltpu
from jax.sharding import PartitionSpec as P

REACH = 2
ROW_BLOCKS = 4
MESH = pl.DeviceIdType.MESH

SIBLING, BACK, PASSED, AHEAD = range(4)


def split(value):
    high = value.astype(jnp.bfloat16)
    return high, (value - high.astype(jnp.float32)).astype(jnp.bfloat16)


def dot_split(first, second):
    left = jnp.concatenate([first[0], first[0], first[1]], axis=1)
    right = jnp.concatenate([second[0], second[1], second[0]], axis=0)
    return jnp.dot(left, right, preferred_element_type=jnp.float32)


def complex_pair(re, im):
    return jnp.concatenate(
        [jnp.concatenate([re, -im], axis=1), jnp.concatenate([im, re], axis=1)], axis=0
    )


def kernel(
    sizes,
    mode_ref, weight_ref, energy_ref, guess_ref,
    green_ref, coupling_ref, onsite_ref, hopping_ref,
    out_ref,
    halo, own, arrived, total, inverse, before, outer,
    coup_hi, coup_lo, coupt_hi, coupt_lo,
    halo_send, halo_recv, kz_send, kz_recv, sp_send, sp_recv,
):
    kz_count, en_count, sp_count = sizes
    energy_count, _, n, _ = green_ref.shape
    ring = kz_count > 2 * REACH
    rows = n // ROW_BLOCKS
    pieces = 2 * ROW_BLOCKS
    k, en, sp = lax.axis_index("kz"), lax.axis_index("en"), lax.axis_index("sp")
    odd = lax.rem(k, 2)
    sibling = k + 1 - 2 * odd
    back = lax.rem(k + kz_count - REACH, kz_count)
    ahead = lax.rem(k + REACH, kz_count)

    barrier = pltpu.get_barrier_semaphore()

    def greet(axis, index):
        pl.semaphore_signal(barrier, inc=1, device_id={axis: index}, device_id_type=MESH)

    greet("kz", sibling)
    greet("kz", back)
    if ring:
        greet("kz", ahead)
    for axis, here, count in (("en", en, en_count), ("sp", sp, sp_count)):
        pl.when(here > 0)(lambda axis=axis, here=here: greet(axis, here - 1))
        pl.when(here < count - 1)(lambda axis=axis, here=here: greet(axis, here + 1))
    expected = 2 + int(ring)
    for here, count in ((en, en_count), (sp, sp_count)):
        expected = expected + (here > 0).astype(jnp.int32) + (here < count - 1).astype(jnp.int32)
    pl.semaphore_wait(barrier, expected)

    def remote(source, target, send, recv, axis, index):
        return pltpu.make_async_remote_copy(
            src_ref=source, dst_ref=target, send_sem=send, recv_sem=recv,
            device_id={axis: index}, device_id_type=MESH,
        )

    def halo_up(p):
        return remote(green_ref.at[energy_count - 1, p], halo.at[0, p],
                      halo_send.at[0, p], halo_recv.at[0, p], "en", en + 1)

    def halo_down(p):
        return remote(green_ref.at[0, p], halo.at[1, p],
                      halo_send.at[1, p], halo_recv.at[1, p], "en", en - 1)

    for p in range(2):
        pl.when(en < en_count - 1)(lambda p=p: halo_up(p).start())
        pl.when(en > 0)(lambda p=p: halo_down(p).start())

    @pl.when(en == 0)
    def _():
        halo[0] = jnp.zeros_like(halo[0])

    @pl.when(en == en_count - 1)
    def _():
        halo[1] = jnp.zeros_like(halo[1])

    def energy_of(i):
        return lax.rem(i + en, energy_count)

    def kz_copy(slot, i, p, source, index):
        return remote(source, arrived.at[slot, i, p], kz_send.at[slot, i, p],
                      kz_recv.at[slot, i, p], "kz", index)

    def to_back(i, p):
        slot = AHEAD if ring else BACK
        return kz_copy(slot, i, p, own.at[i, p], back)

    def to_ahead(i, p):
        return kz_copy(BACK, i, p, own.at[i, p], ahead)

    def to_sibling(i, p):
        return kz_copy(SIBLING, i, p, own.at[i, p], sibling)

    def passing(i, p):
        slot = jnp.where(odd == 1, BACK, AHEAD) if ring else BACK
        return kz_copy(PASSED, i, p, arrived.at[slot, i, p], sibling)

    def issue(i, p):
        e = energy_of(i)

        @pl.when(e > 0)
        def _():
            own[i, p] = green_ref[jnp.maximum(e - 1, 0), p]

        @pl.when(e == 0)
        def _():
            pl.when(en > 0)(lambda: halo_up(p).wait_recv())
            own[i, p] = halo[0, p]

        @pl.when(e < energy_count - 1)
        def _():
            own[i, p] += green_ref[jnp.minimum(e + 1, energy_count - 1), p]

        @pl.when(e == energy_count - 1)
        def _():
            pl.when(en < en_count - 1)(lambda: halo_down(p).wait_recv())
            own[i, p] += halo[1, p]

        to_ahead(i, p).start()
        if ring:
            to_back(i, p).start()
        to_sibling(i, p).start()

    def term(i, p, block, column, first=False):
        mode = mode_ref[column]
        matrix = (coup_hi[mode], coup_lo[mode])
        turned = (coupt_hi[mode], coupt_lo[mode])
        left = dot_split(matrix, split(block)) * weight_ref[mode]
        value = dot_split(split(left), turned)
        if first:
            total[i, p] = value
        else:
            total[i, p] += value

    def own_terms(i, p):
        term(i, p, own[i, p], REACH, first=True)

    def sibling_terms(i, p):
        to_sibling(i, p).wait_recv()
        term(i, p, arrived[SIBLING, i, p], 2 * REACH - 1 - 2 * (1 - odd))

    def pass_on(i, p):
        to_ahead(i, p).wait_recv()
        if ring:
            to_back(i, p).wait_recv()
        passing(i, p).start()

    def far_terms(i, p, between):
        term(i, p, arrived[BACK, i, p], 2 * REACH)
        between()
        term(i, p, arrived[AHEAD if ring else BACK, i, p], 0)
        between()

    def passed_terms(i, p):
        passing(i, p).wait_recv()
        term(i, p, arrived[PASSED, i, p], 2 * REACH - 1 - 2 * odd)

    def link(i, j):
        p, r = j // ROW_BLOCKS, lax.rem(j, ROW_BLOCKS)
        at = pl.ds(pl.multiple_of(r * rows, rows), rows)
        return remote(out_ref.at[energy_of(i), p, at], before.at[i, p, at],
                      sp_send.at[i, j], sp_recv.at[i, j], "sp", sp + 1)

    def chain_step(i, j):
        p, r = j // ROW_BLOCKS, lax.rem(j, ROW_BLOCKS)
        at = pl.ds(pl.multiple_of(r * rows, rows), rows)
        e = energy_of(i)

        @pl.when(sp > 0)
        def _():
            link(i, j).wait_recv()
            out_ref[e, p, at] = outer[at] * before[i, p, at] + inverse[i, p, at]

        @pl.when(sp == 0)
        def _():
            out_ref[e, p, at] = inverse[i, p, at]

        @pl.when(sp < sp_count - 1)
        def _():
            link(i, j).start()

    def invert(i, between):
        e = energy_of(i)
        guess = guess_ref[e]
        shift = onsite_ref[...] - energy_ref[e]
        diagonal = (lax.broadcasted_iota(jnp.int32, (n, n), 0)
                    == lax.broadcasted_iota(jnp.int32, (n, n), 1))
        r_re = jnp.where(diagonal, 1.0 - guess * shift, 0.0) - guess * total[i, 0]
        r_im = -guess * total[i, 1]

        def stack(re, im):
            return tuple(
                jnp.concatenate([a, b], axis=0) for a, b in zip(split(re), split(im))
            )

        def left(re, im):
            return tuple(complex_pair(a, b) for a, b in zip(split(re), split(im)))

        r_left = left(r_re, r_im)
        square = dot_split(r_left, stack(r_re, r_im))
        between()
        s_re, s_im = square[:n], square[n:]
        s_stack = stack(s_re, s_im)
        cube = dot_split(r_left, s_stack)
        fourth = dot_split(left(s_re, s_im), s_stack)
        between()
        one = jnp.where(diagonal, 1.0, 0.0)
        p_re = one + r_re + s_re + cube[:n]
        p_im = r_im + s_im + cube[n:]
        tail = dot_split(left(p_re, p_im), stack(fourth[:n], fourth[n:]))
        inverse[i, 0] = guess * (p_re + tail[:n])
        inverse[i, 1] = guess * (p_im + tail[n:])

    for p in range(2):
        issue(0, p)
    for mode in range(coupling_ref.shape[0]):
        matrix = coupling_ref[mode]
        coup_hi[mode], coup_lo[mode] = split(matrix)
        coupt_hi[mode], coupt_lo[mode] = split(matrix.T)
    across = jnp.broadcast_to(hopping_ref[...], (n, n))
    outer[...] = across * across.T

    pending = []

    def between():
        if pending:
            i, t = pending[0]
            j = t - sp

            @pl.when((sp > 0) & (j >= 0) & (j < pieces))
            def _():
                chain_step(i, j)

            pending[0] = (i, t + 1)

    def finish():
        if pending:
            i, t = pending.pop()

            @pl.loop(t, pieces + sp_count - 1)
            def _(t):
                j = t - sp

                @pl.when((sp > 0) & (j >= 0) & (j < pieces))
                def _():
                    chain_step(i, j)

    for p in range(2):
        own_terms(0, p)
        sibling_terms(0, p)
    for i in range(energy_count):
        last = i == energy_count - 1
        for p in range(2):
            if not last:
                issue(i + 1, p)
            if i == 0 or p == 1:
                pass_on(i, p)
            if not last:
                own_terms(i + 1, p)
            far_terms(i, p, between)
            if not last:
                sibling_terms(i + 1, p)
            passed_terms(i, p)
            between()
        if not last:
            called = []

            def early(i=i, called=called):
                between()
                if called:
                    pass_on(i + 1, 0)
                called.append(1)

            invert(i, early)
            finish()

            @pl.when(sp == 0)
            def _():
                @pl.loop(0, pieces)
                def _(j):
                    chain_step(i, j)

            pending.append((i, 1))
        else:
            invert(i, between)
            finish()

            @pl.loop(0, pieces)
            def _(j):
                chain_step(i, j)

    for p in range(2):
        pl.when(en < en_count - 1)(lambda p=p: halo_up(p).wait_send())
        pl.when(en > 0)(lambda p=p: halo_down(p).wait_send())
    for i in range(energy_count):
        for p in range(2):
            to_ahead(i, p).wait_send()
            if ring:
                to_back(i, p).wait_send()
            to_sibling(i, p).wait_send()
            passing(i, p).wait_send()

        @pl.when(sp < sp_count - 1)
        def _():
            @pl.loop(0, pieces)
            def _(j):
                link(i, j).wait_send()


def body(sizes, green, coupling, phonon_weight, mode_index, onsite, hopping, energies, guess_scale):
    energy_count, n = green.shape[1], green.shape[-1]
    modes = coupling.shape[1]
    blocks = (energy_count, 2, n, n)
    slots = 4 if sizes[0] > 2 * REACH else 3
    pieces = 2 * ROW_BLOCKS
    smem = pl.BlockSpec(memory_space=pltpu.SMEM)
    vmem = pl.BlockSpec(memory_space=pltpu.VMEM)
    half = pltpu.VMEM((modes, n, n), jnp.bfloat16)
    out = pl.pallas_call(
        functools.partial(kernel, sizes),
        out_shape=jax.ShapeDtypeStruct(blocks, jnp.float32),
        in_specs=[smem] * 4 + [vmem] * 4,
        out_specs=vmem,
        scratch_shapes=[
            pltpu.VMEM((2, 2, n, n), jnp.float32),
            pltpu.VMEM(blocks, jnp.float32),
            pltpu.VMEM((slots,) + blocks, jnp.float32),
            pltpu.VMEM(blocks, jnp.float32),
            pltpu.VMEM(blocks, jnp.float32),
            pltpu.VMEM(blocks, jnp.float32),
            pltpu.VMEM((n, n), jnp.float32),
            half, half, half, half,
            pltpu.SemaphoreType.DMA((2, 2)),
            pltpu.SemaphoreType.DMA((2, 2)),
            pltpu.SemaphoreType.DMA((slots, energy_count, 2)),
            pltpu.SemaphoreType.DMA((slots, energy_count, 2)),
            pltpu.SemaphoreType.DMA((energy_count, pieces)),
            pltpu.SemaphoreType.DMA((energy_count, pieces)),
        ],
        compiler_params=pltpu.CompilerParams(
            collective_id=0, has_side_effects=True, vmem_limit_bytes=50 << 20
        ),
    )(
        mode_index[0], phonon_weight, energies, guess_scale.reshape(energy_count),
        green.reshape(blocks), coupling[0], onsite, hopping,
    )
    return out.reshape(1, energy_count, 1, 2, n, n)


def solution(mesh):
    placed = (
        P("kz", "en", "sp", None, None, None),
        P("sp", None, None, None),
        P(),
        P("kz", None),
        P("sp", None),
        P("sp", None),
        P("en"),
        P("kz", "en", "sp"),
    )
    sizes = tuple(mesh.shape[axis] for axis in ("kz", "en", "sp"))
    return jax.shard_map(
        functools.partial(body, sizes),
        mesh=mesh,
        in_specs=placed,
        out_specs=P("kz", "en", "sp", None, None, None),
        check_vma=False,
    )
```

```python
import functools

import jax
import jax.numpy as jnp
from jax import lax
from jax.experimental import pallas as pl
from jax.experimental.pallas import tpu as pltpu
from jax.sharding import PartitionSpec as P

REACH = 2
ROW_BLOCKS = 8
SHARES = 2
PACE = 2
MESH = pl.DeviceIdType.MESH

SIBLING, BACK, PASSED, AHEAD = range(4)


def split(value):
    high = value.astype(jnp.bfloat16)
    return high, (value - high.astype(jnp.float32)).astype(jnp.bfloat16)


def dot_split(first, second):
    left = jnp.concatenate([first[0], first[0], first[1]], axis=1)
    right = jnp.concatenate([second[0], second[1], second[0]], axis=0)
    return jnp.dot(left, right, preferred_element_type=jnp.float32)


def complex_pair(re, im):
    return jnp.concatenate(
        [jnp.concatenate([re, -im], axis=1), jnp.concatenate([im, re], axis=1)], axis=0
    )


def kernel(
    sizes,
    mode_in, weight_in, energy_in, guess_in, green_in, coupling_in, onsite_in, hopping_in,
    out_ref,
    mode_ref, weight_ref, energy_ref, guess_ref, green_ref, coupling_ref, onsite_ref, hopping_ref,
    halo, own, arrived, total, inverse, before, outer,
    coup_hi, coup_lo, coupt_hi, coupt_lo,
    small_sem, coupling_sem, green_sem, halo_send, halo_recv, kz_send, kz_recv, sp_send, sp_recv,
):
    kz_count, en_count, sp_count = sizes
    energy_count, _, n, _ = green_ref.shape
    ring = kz_count > 2 * REACH
    rows = n // ROW_BLOCKS
    share = n // SHARES
    pieces = 2 * ROW_BLOCKS
    k, en, sp = lax.axis_index("kz"), lax.axis_index("en"), lax.axis_index("sp")
    odd = lax.rem(k, 2)
    sibling = k + 1 - 2 * odd
    back = lax.rem(k + kz_count - REACH, kz_count)
    ahead = lax.rem(k + REACH, kz_count)

    def green_load(e, p):
        return pltpu.make_async_copy(green_in.at[e, p], green_ref.at[e, p], green_sem.at[e, p])

    for p in range(2):
        for e in range(energy_count):
            green_load(e, p).start()
    small_loads = [
        pltpu.make_async_copy(source, target, small_sem.at[index])
        for index, (source, target) in enumerate((
            (mode_in, mode_ref), (weight_in, weight_ref), (energy_in, energy_ref),
            (guess_in, guess_ref), (onsite_in, onsite_ref), (hopping_in, hopping_ref),
        ))
    ]
    coupling_load = pltpu.make_async_copy(coupling_in, coupling_ref, coupling_sem)
    for load in small_loads + [coupling_load]:
        load.start()

    barrier = pltpu.get_barrier_semaphore()

    def greet(axis, index):
        pl.semaphore_signal(barrier, inc=1, device_id={axis: index}, device_id_type=MESH)

    greet("kz", sibling)
    greet("kz", back)
    if ring:
        greet("kz", ahead)
    for axis, here, count in (("en", en, en_count), ("sp", sp, sp_count)):
        pl.when(here > 0)(lambda axis=axis, here=here: greet(axis, here - 1))
        pl.when(here < count - 1)(lambda axis=axis, here=here: greet(axis, here + 1))
    expected = 2 + int(ring)
    for here, count in ((en, en_count), (sp, sp_count)):
        expected = expected + (here > 0).astype(jnp.int32) + (here < count - 1).astype(jnp.int32)
    pl.semaphore_wait(barrier, expected)

    def remote(source, target, send, recv, axis, index):
        return pltpu.make_async_remote_copy(
            src_ref=source, dst_ref=target, send_sem=send, recv_sem=recv,
            device_id={axis: index}, device_id_type=MESH,
        )

    def halo_up(p):
        return remote(green_in.at[energy_count - 1, p], halo.at[0, p],
                      halo_send.at[0, p], halo_recv.at[0, p], "en", en + 1)

    def halo_down(p):
        return remote(green_in.at[0, p], halo.at[1, p],
                      halo_send.at[1, p], halo_recv.at[1, p], "en", en - 1)

    for p in range(2):
        pl.when(en < en_count - 1)(lambda p=p: halo_up(p).start())
        pl.when(en > 0)(lambda p=p: halo_down(p).start())

    @pl.when(en == 0)
    def _():
        halo[0] = jnp.zeros_like(halo[0])

    @pl.when(en == en_count - 1)
    def _():
        halo[1] = jnp.zeros_like(halo[1])

    def energy_of(i):
        return lax.rem(i + en, energy_count)

    def kz_copy(slot, i, p, h, source, index):
        at = pl.ds(h * share, share)
        return remote(source.at[i, p, at], arrived.at[slot, i, p, at], kz_send.at[slot, i, p, h],
                      kz_recv.at[slot, i, p, h], "kz", index)

    def to_back(i, p, h):
        return kz_copy(AHEAD if ring else BACK, i, p, h, own, back)

    def to_ahead(i, p, h):
        return kz_copy(BACK, i, p, h, own, ahead)

    def to_sibling(i, p, h):
        return kz_copy(SIBLING, i, p, h, own, sibling)

    def passing(i, p, h):
        slot = jnp.where(odd == 1, BACK, AHEAD) if ring else BACK
        return kz_copy(PASSED, i, p, h, arrived.at[slot], sibling)

    def issue(i, p):
        e = energy_of(i)
        if i == 0:
            for other in range(energy_count):
                green_load(other, p).wait()

        @pl.when(e > 0)
        def _():
            own[i, p] = green_ref[jnp.maximum(e - 1, 0), p]

        @pl.when(e == 0)
        def _():
            pl.when(en > 0)(lambda: halo_up(p).wait_recv())
            own[i, p] = halo[0, p]

        @pl.when(e < energy_count - 1)
        def _():
            own[i, p] += green_ref[jnp.minimum(e + 1, energy_count - 1), p]

        @pl.when(e == energy_count - 1)
        def _():
            pl.when(en < en_count - 1)(lambda: halo_down(p).wait_recv())
            own[i, p] += halo[1, p]

        for h in range(SHARES):
            to_ahead(i, p, h).start()
            if ring:
                to_back(i, p, h).start()
        for h in range(SHARES):
            to_sibling(i, p, h).start()

    def term(i, p, block, column, first=False):
        mode = mode_ref[column]
        matrix = (coup_hi[mode], coup_lo[mode])
        turned = (coupt_hi[mode], coupt_lo[mode])
        left = dot_split(matrix, split(block)) * weight_ref[mode]
        value = dot_split(split(left), turned)
        if first:
            total[i, p] = value
        else:
            total[i, p] += value

    def own_terms(i, p):
        term(i, p, own[i, p], REACH, first=True)

    def sibling_terms(i, p):
        for h in range(SHARES):
            to_sibling(i, p, h).wait_recv()
        term(i, p, arrived[SIBLING, i, p], 2 * REACH - 1 - 2 * (1 - odd))

    def pass_on(i, p):
        for h in range(SHARES):
            to_ahead(i, p, h).wait_recv()
            if ring:
                to_back(i, p, h).wait_recv()
            passing(i, p, h).start()

    def far_terms(i, p, between):
        term(i, p, arrived[BACK, i, p], 2 * REACH)
        between()
        term(i, p, arrived[AHEAD if ring else BACK, i, p], 0)
        between()

    def passed_terms(i, p):
        for h in range(SHARES):
            passing(i, p, h).wait_recv()
        term(i, p, arrived[PASSED, i, p], 2 * REACH - 1 - 2 * odd)

    def link(i, j):
        p, r = j // ROW_BLOCKS, lax.rem(j, ROW_BLOCKS)
        at = pl.ds(pl.multiple_of(r * rows, rows), rows)
        return remote(out_ref.at[energy_of(i), p, at], before.at[i, p, at],
                      sp_send.at[i, j], sp_recv.at[i, j], "sp", sp + 1)

    def chain_step(i, j):
        p, r = j // ROW_BLOCKS, lax.rem(j, ROW_BLOCKS)
        at = pl.ds(pl.multiple_of(r * rows, rows), rows)
        e = energy_of(i)

        @pl.when(sp > 0)
        def _():
            link(i, j).wait_recv()
            out_ref[e, p, at] = outer[at] * before[i, p, at] + inverse[i, p, at]

        @pl.when(sp == 0)
        def _():
            out_ref[e, p, at] = inverse[i, p, at]

        @pl.when(sp < sp_count - 1)
        def _():
            link(i, j).start()

    def invert(i, between, emit):
        e = energy_of(i)
        guess = guess_ref[e]
        shift = onsite_ref[...] - energy_ref[e]
        diagonal = (lax.broadcasted_iota(jnp.int32, (n, n), 0)
                    == lax.broadcasted_iota(jnp.int32, (n, n), 1))
        r_re = jnp.where(diagonal, 1.0 - guess * shift, 0.0) - guess * total[i, 0]
        r_im = -guess * total[i, 1]

        def stack(re, im):
            return tuple(
                jnp.concatenate([a, b], axis=0) for a, b in zip(split(re), split(im))
            )

        def left(re, im):
            return tuple(complex_pair(a, b) for a, b in zip(split(re), split(im)))

        r_left = left(r_re, r_im)
        square = dot_split(r_left, stack(r_re, r_im))
        between()
        s_re, s_im = square[:n], square[n:]
        s_stack = stack(s_re, s_im)
        cube = dot_split(r_left, s_stack)
        fourth = dot_split(left(s_re, s_im), s_stack)
        between()
        one = jnp.where(diagonal, 1.0, 0.0)
        p_re = one + r_re + s_re + cube[:n]
        p_im = r_im + s_im + cube[n:]
        re, im = split(p_re), split(p_im)
        fourth = stack(fourth[:n], fourth[n:])
        sides = [(a, -b) for a, b in zip(re, im)], list(zip(im, re))
        for p, (side, whole) in enumerate(zip(sides, (p_re, p_im))):
            rows_left = tuple(jnp.concatenate(pair, axis=1) for pair in side)
            inverse[i, p] = guess * (whole + dot_split(rows_left, fourth))
            emit(p)

    for p in range(2):
        issue(0, p)
    for load in small_loads + [coupling_load]:
        load.wait()
    for mode in range(coupling_ref.shape[0]):
        matrix = coupling_ref[mode]
        coup_hi[mode], coup_lo[mode] = split(matrix)
        coupt_hi[mode], coupt_lo[mode] = split(matrix.T)
    across = jnp.broadcast_to(hopping_ref[...], (n, n))
    outer[...] = across * across.T

    pending = []

    def paced(i, t):
        group = t - sp

        @pl.when((sp > 0) & (group >= 0) & (group < pieces // PACE))
        def _():
            for step in range(PACE):
                chain_step(i, group * PACE + step)

    def between():
        if pending:
            i, t = pending[0]
            paced(i, t)
            pending[0] = (i, t + 1)

    def finish():
        if pending:
            i, t = pending.pop()

            @pl.loop(t, pieces // PACE + sp_count - 1)
            def _(t):
                paced(i, t)

    def chain_part(i, p):
        @pl.loop(p * ROW_BLOCKS, (p + 1) * ROW_BLOCKS)
        def _(j):
            chain_step(i, j)

    for p in range(2):
        own_terms(0, p)
        sibling_terms(0, p)
    for i in range(energy_count):
        last = i == energy_count - 1
        for p in range(2):
            if not last:
                issue(i + 1, p)
            if i == 0 or p == 1:
                pass_on(i, p)
            if not last:
                own_terms(i + 1, p)
            far_terms(i, p, between)
            if not last:
                sibling_terms(i + 1, p)
            passed_terms(i, p)
            between()
        if not last:
            called = []

            def early(i=i, called=called):
                between()
                if called:
                    pass_on(i + 1, 0)
                called.append(1)

            def emit(p, i=i):
                if p == 0:
                    finish()
                pl.when(sp == 0)(lambda: chain_part(i, p))

            invert(i, early, emit)
            pending.append((i, 1))
        else:

            def emit(p, i=i):
                if p == 0:
                    finish()
                chain_part(i, p)

            invert(i, between, emit)

    for p in range(2):
        pl.when(en < en_count - 1)(lambda p=p: halo_up(p).wait_send())
        pl.when(en > 0)(lambda p=p: halo_down(p).wait_send())
    for i in range(energy_count):
        for p in range(2):
            for h in range(SHARES):
                to_ahead(i, p, h).wait_send()
                if ring:
                    to_back(i, p, h).wait_send()
                to_sibling(i, p, h).wait_send()
                passing(i, p, h).wait_send()

        @pl.when(sp < sp_count - 1)
        def _():
            @pl.loop(0, pieces)
            def _(j):
                link(i, j).wait_send()


def body(sizes, green, coupling, phonon_weight, mode_index, onsite, hopping, energies, guess_scale):
    energy_count, n = green.shape[1], green.shape[-1]
    modes = coupling.shape[1]
    blocks = (energy_count, 2, n, n)
    slots = 4 if sizes[0] > 2 * REACH else 3
    pieces = 2 * ROW_BLOCKS
    hbm = pl.BlockSpec(memory_space=pltpu.HBM)
    vmem = pl.BlockSpec(memory_space=pltpu.VMEM)
    half = pltpu.VMEM((modes, n, n), jnp.bfloat16)
    out = pl.pallas_call(
        functools.partial(kernel, sizes),
        out_shape=jax.ShapeDtypeStruct(blocks, jnp.float32),
        in_specs=[hbm] * 8,
        out_specs=vmem,
        scratch_shapes=[
            pltpu.SMEM(mode_index.shape[1:], jnp.int32),
            pltpu.SMEM(phonon_weight.shape, jnp.float32),
            pltpu.SMEM((energy_count,), jnp.float32),
            pltpu.SMEM((energy_count,), jnp.float32),
            pltpu.VMEM(blocks, jnp.float32),
            pltpu.VMEM(coupling.shape[1:], jnp.float32),
            pltpu.VMEM((1, n), jnp.float32),
            pltpu.VMEM((1, n), jnp.float32),
            pltpu.VMEM((2, 2, n, n), jnp.float32),
            pltpu.VMEM(blocks, jnp.float32),
            pltpu.VMEM((slots,) + blocks, jnp.float32),
            pltpu.VMEM(blocks, jnp.float32),
            pltpu.VMEM(blocks, jnp.float32),
            pltpu.VMEM(blocks, jnp.float32),
            pltpu.VMEM((n, n), jnp.float32),
            half, half, half, half,
            pltpu.SemaphoreType.DMA((6,)),
            pltpu.SemaphoreType.DMA,
            pltpu.SemaphoreType.DMA((energy_count, 2)),
            pltpu.SemaphoreType.DMA((2, 2)),
            pltpu.SemaphoreType.DMA((2, 2)),
            pltpu.SemaphoreType.DMA((slots, energy_count, 2, SHARES)),
            pltpu.SemaphoreType.DMA((slots, energy_count, 2, SHARES)),
            pltpu.SemaphoreType.DMA((energy_count, pieces)),
            pltpu.SemaphoreType.DMA((energy_count, pieces)),
        ],
        compiler_params=pltpu.CompilerParams(
            collective_id=0, has_side_effects=True, vmem_limit_bytes=67_043_328
        ),
    )(
        mode_index[0], phonon_weight, energies, guess_scale.reshape(energy_count),
        green.reshape(blocks), coupling[0], onsite, hopping,
    )
    return out.reshape(1, energy_count, 1, 2, n, n)


def solution(mesh):
    placed = (
        P("kz", "en", "sp", None, None, None),
        P("sp", None, None, None),
        P(),
        P("kz", None),
        P("sp", None),
        P("sp", None),
        P("en"),
        P("kz", "en", "sp"),
    )
    sizes = tuple(mesh.shape[axis] for axis in ("kz", "en", "sp"))
    return jax.shard_map(
        functools.partial(body, sizes),
        mesh=mesh,
        in_specs=placed,
        out_specs=P("kz", "en", "sp", None, None, None),
        check_vma=False,
    )
```

```python
import functools

import jax
import jax.numpy as jnp
from jax import lax
from jax.experimental import pallas as pl
from jax.experimental.pallas import tpu as pltpu
from jax.sharding import PartitionSpec as P

REACH = 2
ROW_BLOCKS = 8
SHARES = 2
PACE = 2
WAITING = 2
MESH = pl.DeviceIdType.MESH

SIBLING, BACK, PASSED, AHEAD = range(4)


def split(value):
    high = value.astype(jnp.bfloat16)
    return high, (value - high.astype(jnp.float32)).astype(jnp.bfloat16)


def dot_split(first, second):
    left = jnp.concatenate([first[0], first[0], first[1]], axis=1)
    right = jnp.concatenate([second[0], second[1], second[0]], axis=0)
    return jnp.dot(left, right, preferred_element_type=jnp.float32)


def complex_pair(re, im):
    return jnp.concatenate(
        [jnp.concatenate([re, -im], axis=1), jnp.concatenate([im, re], axis=1)], axis=0
    )


def kernel(
    sizes,
    mode_in, weight_in, energy_in, guess_in, green_in, coupling_in, onsite_in, hopping_in,
    out_ref,
    mode_ref, weight_ref, energy_ref, guess_ref, green_ref, coupling_ref, onsite_ref, hopping_ref,
    halo, own, arrived, total, inverse, before, outer,
    coup_hi, coup_lo, coupt_hi, coupt_lo,
    small_sem, coupling_sem, green_sem, halo_send, halo_recv, kz_send, kz_recv, sp_send, sp_recv,
):
    kz_count, en_count, sp_count = sizes
    energy_count, _, n, _ = green_ref.shape
    ring = kz_count > 2 * REACH
    rows = n // ROW_BLOCKS
    share = n // SHARES
    pieces = 2 * ROW_BLOCKS
    k, en, sp = lax.axis_index("kz"), lax.axis_index("en"), lax.axis_index("sp")
    odd = lax.rem(k, 2)
    sibling = k + 1 - 2 * odd
    back = lax.rem(k + kz_count - REACH, kz_count)
    ahead = lax.rem(k + REACH, kz_count)

    def green_load(e, p):
        return pltpu.make_async_copy(green_in.at[e, p], green_ref.at[e, p], green_sem.at[e, p])

    for p in range(2):
        for e in range(energy_count):
            green_load(e, p).start()
    small_loads = [
        pltpu.make_async_copy(source, target, small_sem.at[index])
        for index, (source, target) in enumerate((
            (mode_in, mode_ref), (weight_in, weight_ref), (energy_in, energy_ref),
            (guess_in, guess_ref), (onsite_in, onsite_ref), (hopping_in, hopping_ref),
        ))
    ]
    coupling_load = pltpu.make_async_copy(coupling_in, coupling_ref, coupling_sem)
    for load in small_loads + [coupling_load]:
        load.start()

    barrier = pltpu.get_barrier_semaphore()

    def greet(axis, index):
        pl.semaphore_signal(barrier, inc=1, device_id={axis: index}, device_id_type=MESH)

    greet("kz", sibling)
    greet("kz", back)
    if ring:
        greet("kz", ahead)
    for axis, here, count in (("en", en, en_count), ("sp", sp, sp_count)):
        pl.when(here > 0)(lambda axis=axis, here=here: greet(axis, here - 1))
        pl.when(here < count - 1)(lambda axis=axis, here=here: greet(axis, here + 1))
    expected = 2 + int(ring)
    for here, count in ((en, en_count), (sp, sp_count)):
        expected = expected + (here > 0).astype(jnp.int32) + (here < count - 1).astype(jnp.int32)
    pl.semaphore_wait(barrier, expected)

    def remote(source, target, send, recv, axis, index):
        return pltpu.make_async_remote_copy(
            src_ref=source, dst_ref=target, send_sem=send, recv_sem=recv,
            device_id={axis: index}, device_id_type=MESH,
        )

    def halo_up(p):
        return remote(green_in.at[energy_count - 1, p], halo.at[0, p],
                      halo_send.at[0, p], halo_recv.at[0, p], "en", en + 1)

    def halo_down(p):
        return remote(green_in.at[0, p], halo.at[1, p],
                      halo_send.at[1, p], halo_recv.at[1, p], "en", en - 1)

    for p in range(2):
        pl.when(en < en_count - 1)(lambda p=p: halo_up(p).start())
        pl.when(en > 0)(lambda p=p: halo_down(p).start())

    @pl.when(en == 0)
    def _():
        halo[0] = jnp.zeros_like(halo[0])

    @pl.when(en == en_count - 1)
    def _():
        halo[1] = jnp.zeros_like(halo[1])

    def energy_of(i):
        return lax.rem(i + en, energy_count)

    def kz_copy(slot, i, p, h, source, index):
        at = pl.ds(h * share, share)
        return remote(source.at[i, p, at], arrived.at[slot, i, p, at], kz_send.at[slot, i, p, h],
                      kz_recv.at[slot, i, p, h], "kz", index)

    def to_back(i, p, h):
        return kz_copy(AHEAD if ring else BACK, i, p, h, own, back)

    def to_ahead(i, p, h):
        return kz_copy(BACK, i, p, h, own, ahead)

    def to_sibling(i, p, h):
        return kz_copy(SIBLING, i, p, h, own, sibling)

    def passing(i, p, h):
        slot = jnp.where(odd == 1, BACK, AHEAD) if ring else BACK
        return kz_copy(PASSED, i, p, h, arrived.at[slot], sibling)

    def issue(i, p):
        e = energy_of(i)
        if i == 0:
            for other in range(energy_count):
                green_load(other, p).wait()

        @pl.when(e > 0)
        def _():
            own[i, p] = green_ref[jnp.maximum(e - 1, 0), p]

        @pl.when(e == 0)
        def _():
            pl.when(en > 0)(lambda: halo_up(p).wait_recv())
            own[i, p] = halo[0, p]

        @pl.when(e < energy_count - 1)
        def _():
            own[i, p] += green_ref[jnp.minimum(e + 1, energy_count - 1), p]

        @pl.when(e == energy_count - 1)
        def _():
            pl.when(en < en_count - 1)(lambda: halo_down(p).wait_recv())
            own[i, p] += halo[1, p]

        for h in range(SHARES):
            to_ahead(i, p, h).start()
            if ring:
                to_back(i, p, h).start()
        for h in range(SHARES):
            to_sibling(i, p, h).start()

    def term(i, p, block, column, first=False):
        mode = mode_ref[column]
        matrix = (coup_hi[mode], coup_lo[mode])
        turned = (coupt_hi[mode], coupt_lo[mode])
        left = dot_split(matrix, split(block)) * weight_ref[mode]
        value = dot_split(split(left), turned)
        if first:
            total[i, p] = value
        else:
            total[i, p] += value

    def own_terms(i, p):
        term(i, p, own[i, p], REACH, first=True)

    def sibling_terms(i, p):
        for h in range(SHARES):
            to_sibling(i, p, h).wait_recv()
        term(i, p, arrived[SIBLING, i, p], 2 * REACH - 1 - 2 * (1 - odd))

    def pass_on(i, p):
        for h in range(SHARES):
            to_ahead(i, p, h).wait_recv()
            if ring:
                to_back(i, p, h).wait_recv()
            passing(i, p, h).start()

    def far_terms(i, p, between):
        term(i, p, arrived[BACK, i, p], 2 * REACH)
        between()
        term(i, p, arrived[AHEAD if ring else BACK, i, p], 0)
        between()

    def passed_terms(i, p):
        for h in range(SHARES):
            passing(i, p, h).wait_recv()
        term(i, p, arrived[PASSED, i, p], 2 * REACH - 1 - 2 * odd)

    def link(i, j):
        p, r = j // ROW_BLOCKS, lax.rem(j, ROW_BLOCKS)
        at = pl.ds(pl.multiple_of(r * rows, rows), rows)
        return remote(out_ref.at[energy_of(i), p, at], before.at[i, p, at],
                      sp_send.at[i, j], sp_recv.at[i, j], "sp", sp + 1)

    def chain_step(i, j):
        p, r = j // ROW_BLOCKS, lax.rem(j, ROW_BLOCKS)
        at = pl.ds(pl.multiple_of(r * rows, rows), rows)
        e = energy_of(i)

        @pl.when(sp > 0)
        def _():
            link(i, j).wait_recv()
            out_ref[e, p, at] = outer[at] * before[i, p, at] + inverse[i, p, at]

        @pl.when(sp == 0)
        def _():
            out_ref[e, p, at] = inverse[i, p, at]

        @pl.when(sp < sp_count - 1)
        def _():
            link(i, j).start()

    def invert(i, between, emit):
        e = energy_of(i)
        guess = guess_ref[e]
        shift = onsite_ref[...] - energy_ref[e]
        diagonal = (lax.broadcasted_iota(jnp.int32, (n, n), 0)
                    == lax.broadcasted_iota(jnp.int32, (n, n), 1))
        r_re = jnp.where(diagonal, 1.0 - guess * shift, 0.0) - guess * total[i, 0]
        r_im = -guess * total[i, 1]

        def stack(re, im):
            return tuple(
                jnp.concatenate([a, b], axis=0) for a, b in zip(split(re), split(im))
            )

        def left(re, im):
            return tuple(complex_pair(a, b) for a, b in zip(split(re), split(im)))

        r_left = left(r_re, r_im)
        square = dot_split(r_left, stack(r_re, r_im))
        between()
        s_re, s_im = square[:n], square[n:]
        s_stack = stack(s_re, s_im)
        cube = dot_split(r_left, s_stack)
        fourth = dot_split(left(s_re, s_im), s_stack)
        between()
        one = jnp.where(diagonal, 1.0, 0.0)
        p_re = one + r_re + s_re + cube[:n]
        p_im = r_im + s_im + cube[n:]
        re, im = split(p_re), split(p_im)
        fourth = stack(fourth[:n], fourth[n:])
        sides = [(a, -b) for a, b in zip(re, im)], list(zip(im, re))
        for p, (side, whole) in enumerate(zip(sides, (p_re, p_im))):
            rows_left = tuple(jnp.concatenate(pair, axis=1) for pair in side)
            inverse[i, p] = guess * (whole + dot_split(rows_left, fourth))
            emit(p)

    for p in range(2):
        issue(0, p)
    for load in small_loads + [coupling_load]:
        load.wait()
    for mode in range(coupling_ref.shape[0]):
        matrix = coupling_ref[mode]
        coup_hi[mode], coup_lo[mode] = split(matrix)
        coupt_hi[mode], coupt_lo[mode] = split(matrix.T)
    across = jnp.broadcast_to(hopping_ref[...], (n, n))
    outer[...] = across * across.T

    pending = []

    def paced(i, t):
        group = t - sp

        @pl.when((sp > 0) & (group >= 0) & (group < pieces // PACE))
        def _():
            for step in range(PACE):
                chain_step(i, group * PACE + step)

    def between():
        if pending:
            i, t = pending[0]
            paced(i, t)
            pending[0] = (i, t + 1)

    def finish():
        if pending:
            i, t = pending.pop()

            @pl.loop(t, pieces // PACE + sp_count - 1)
            def _(t):
                paced(i, t)

    def chain_part(i, p):
        @pl.loop(p * ROW_BLOCKS, (p + 1) * ROW_BLOCKS)
        def _(j):
            chain_step(i, j)

    for p in range(2):
        own_terms(0, p)
        sibling_terms(0, p)
    for i in range(energy_count):
        last = i == energy_count - 1
        for p in range(2):
            if not last:
                issue(i + 1, p)
            if i > 0 and p == 1:
                for _ in range(WAITING):
                    between()
            if i == 0 or p == 1:
                pass_on(i, p)
            if not last:
                own_terms(i + 1, p)
            far_terms(i, p, between)
            if not last:
                sibling_terms(i + 1, p)
            passed_terms(i, p)
            between()
        if not last:
            called = []

            def early(i=i, called=called):
                between()
                if called:
                    pass_on(i + 1, 0)
                called.append(1)

            def emit(p, i=i):
                if p == 0:
                    finish()
                pl.when(sp == 0)(lambda: chain_part(i, p))

            invert(i, early, emit)
            pending.append((i, 1))
        else:

            def emit(p, i=i):
                if p == 0:
                    finish()
                chain_part(i, p)

            invert(i, between, emit)

    for p in range(2):
        pl.when(en < en_count - 1)(lambda p=p: halo_up(p).wait_send())
        pl.when(en > 0)(lambda p=p: halo_down(p).wait_send())
    for i in range(energy_count):
        for p in range(2):
            for h in range(SHARES):
                to_ahead(i, p, h).wait_send()
                if ring:
                    to_back(i, p, h).wait_send()
                to_sibling(i, p, h).wait_send()
                passing(i, p, h).wait_send()

        @pl.when(sp < sp_count - 1)
        def _():
            @pl.loop(0, pieces)
            def _(j):
                link(i, j).wait_send()


def body(sizes, green, coupling, phonon_weight, mode_index, onsite, hopping, energies, guess_scale):
    energy_count, n = green.shape[1], green.shape[-1]
    modes = coupling.shape[1]
    blocks = (energy_count, 2, n, n)
    slots = 4 if sizes[0] > 2 * REACH else 3
    pieces = 2 * ROW_BLOCKS
    hbm = pl.BlockSpec(memory_space=pltpu.HBM)
    vmem = pl.BlockSpec(memory_space=pltpu.VMEM)
    half = pltpu.VMEM((modes, n, n), jnp.bfloat16)
    out = pl.pallas_call(
        functools.partial(kernel, sizes),
        out_shape=jax.ShapeDtypeStruct(blocks, jnp.float32),
        in_specs=[hbm] * 8,
        out_specs=vmem,
        scratch_shapes=[
            pltpu.SMEM(mode_index.shape[1:], jnp.int32),
            pltpu.SMEM(phonon_weight.shape, jnp.float32),
            pltpu.SMEM((energy_count,), jnp.float32),
            pltpu.SMEM((energy_count,), jnp.float32),
            pltpu.VMEM(blocks, jnp.float32),
            pltpu.VMEM(coupling.shape[1:], jnp.float32),
            pltpu.VMEM((1, n), jnp.float32),
            pltpu.VMEM((1, n), jnp.float32),
            pltpu.VMEM((2, 2, n, n), jnp.float32),
            pltpu.VMEM(blocks, jnp.float32),
            pltpu.VMEM((slots,) + blocks, jnp.float32),
            pltpu.VMEM(blocks, jnp.float32),
            pltpu.VMEM(blocks, jnp.float32),
            pltpu.VMEM(blocks, jnp.float32),
            pltpu.VMEM((n, n), jnp.float32),
            half, half, half, half,
            pltpu.SemaphoreType.DMA((6,)),
            pltpu.SemaphoreType.DMA,
            pltpu.SemaphoreType.DMA((energy_count, 2)),
            pltpu.SemaphoreType.DMA((2, 2)),
            pltpu.SemaphoreType.DMA((2, 2)),
            pltpu.SemaphoreType.DMA((slots, energy_count, 2, SHARES)),
            pltpu.SemaphoreType.DMA((slots, energy_count, 2, SHARES)),
            pltpu.SemaphoreType.DMA((energy_count, pieces)),
            pltpu.SemaphoreType.DMA((energy_count, pieces)),
        ],
        compiler_params=pltpu.CompilerParams(
            collective_id=0, has_side_effects=True, vmem_limit_bytes=50 << 20
        ),
    )(
        *(
            pltpu.with_memory_space_constraint(value, pltpu.HBM)
            for value in (
                mode_index[0], phonon_weight, energies, guess_scale.reshape(energy_count),
                green.reshape(blocks), coupling[0], onsite, hopping,
            )
        )
    )
    return out.reshape(1, energy_count, 1, 2, n, n)


def solution(mesh):
    placed = (
        P("kz", "en", "sp", None, None, None),
        P("sp", None, None, None),
        P(),
        P("kz", None),
        P("sp", None),
        P("sp", None),
        P("en"),
        P("kz", "en", "sp"),
    )
    sizes = tuple(mesh.shape[axis] for axis in ("kz", "en", "sp"))
    return jax.shard_map(
        functools.partial(body, sizes),
        mesh=mesh,
        in_specs=placed,
        out_specs=P("kz", "en", "sp", None, None, None),
        check_vma=False,
    )
```
